32 devices in a mesh: clip: 2 (over y), height: 4 (over z), head: 4 (over x, core).
Axes of the slice: x: 2, y: 2, z: 4, core: 2. Of those that a mesh axis runs over, the one named last changes fastest.
Arguments:
- tokens: bfloat16 [8, 192, 5120], P(('clip', 'height'), None, 'head'), parts along dimension 0, may hold values from -6 to 6
- in_sign: int32 [5120], replicated, may hold values from 0 to 1
- qkv_codes: int32 [640, 3, 3072], P(None, None, 'head'), may hold values from 0 to 65535
- qkv_scale: float32 [3, 3072], P(None, 'head'), may hold values from 0.3 to 3
- qkv_sign: int32 [3, 3072], P(None, 'head'), may hold values from 0 to 1
- windows: int32 [8, 3, 27], P(('clip', 'height')), parts along dimension 0, may hold values from 0 to 11, as said below
- oin_sign: int32 [3072], P('head'), may hold values from 0 to 1
- out_codes: int32 [384, 5120], P('head'), may hold values from 0 to 65535
- out_scale: float32 [5120], replicated, may hold values from 2 to 20
- out_sign: int32 [5120], replicated, may hold values from 0 to 1
Outputs:
- attention_out: bfloat16 [8, 192, 5120], P(('clip', 'height'), 'head'), parts along dimension 0
The draws below stay inside these ranges and needn't reach their ends.
There are 2 independent parts, one for each index of `clip`. The reference program is written for one: setup_inputs(seed, part) draws one part's arguments, and reference() takes and returns one part's arrays. A program takes and returns all parts, laid end to end along the dimension named above; an argument that names none is the same for every part. Nothing has to cross between parts.
Inputs may be any that keep to these rules, and one draw needn't show every extreme that they name: `windows`: each row lists the query tile itself and 26 further entries, each one of the 27 tiles of the 3 x 3 x 3 block of tiles centred on the query tile (each of the three coordinates clipped into the grid of 1 x 4 x 3 tiles); entries may repeat and appear in any order.
All inputs are finite; a program needn't handle non-finite values.
Results may differ from the reference program's by a relative error of at most 0.015.
Values may be sent and summed in bfloat16 or wider, within the bound.
A program may use at most 128 MiB of HBM per device.

```python
import math
import jax
import jax.numpy as jnp
import numpy as np
from jax import lax

D = 5120
HD = 128
HEADS = 24
HAD = 128
HROWS = 4
WTILES = 3
TTILES = 1
SLABS = 4
TILE = 64
QTILES = 3
TOK_DEV = 192
TOKENS = 768
N_HEAD = 4


def draw_windows(key, part):
    slab_index = jnp.arange(SLABS, dtype=jnp.int32)[:, None, None, None, None]
    col_index = jnp.arange(WTILES, dtype=jnp.int32)[None, :, None, None, None]
    stepping = jnp.arange(3, dtype=jnp.int32) - 1
    time_all = jnp.clip(slab_index // HROWS + stepping[None, None, :, None, None], 0, TTILES - 1)
    row_all = jnp.clip(slab_index % HROWS + stepping[None, None, None, :, None], 0, HROWS - 1)
    col_all = jnp.clip(col_index + stepping[None, None, None, None, :], 0, WTILES - 1)
    tile_ids = ((time_all * HROWS + row_all) * WTILES + col_all).reshape(SLABS * WTILES, 27)
    pick_key = jax.random.fold_in(key, 11)
    order_key = jax.random.fold_in(key, 23)
    picks = jax.random.randint(pick_key, (SLABS * WTILES, 27), 0, 27).astype(jnp.int32)
    picks = picks.at[:, 0].set(13)
    chosen = jnp.take_along_axis(tile_ids, picks, axis=1)
    row_keys = jax.random.split(order_key, SLABS * WTILES)
    orders = jax.vmap(lambda one_key: jax.random.permutation(one_key, 27))(row_keys)
    shuffled = jnp.take_along_axis(chosen, orders.astype(jnp.int32), axis=1)
    return shuffled.reshape(SLABS, WTILES, 27).astype(jnp.int32)


def with_ends(entries, own_key, low, high):
    spot = [jax.random.randint(jax.random.fold_in(own_key, axis), (), 0, length) for axis, length in enumerate(entries.shape)]
    widest = entries.shape.index(max(entries.shape))
    next_to = spot[:widest] + [(spot[widest] + 1) % entries.shape[widest]] + spot[widest + 1:]
    return entries.at[tuple(spot)].set(low).at[tuple(next_to)].set(high)


def block_scale(stream_key, shape, shards, smallest, top_value):
    def one(position, blocks):
        heights = jax.random.uniform(jax.random.fold_in(jax.random.fold_in(stream_key, 6), position), (blocks,), jnp.float32, smallest / len(shards), top_value / len(shards))
        return jnp.repeat(jnp.exp(heights), shape[position] // blocks).reshape((-1,) + (1,) * (len(shape) - position - 1))

    level = one(*shards[0])
    for cut in shards[1:]:
        level = level * one(*cut)
    return level


def centred(stream_key, shape, deviation, limit, cuts=(), held_as=jnp.bfloat16):
    values = jax.random.normal(stream_key, shape, jnp.float32) * deviation
    if len(cuts) > 0:
        values = block_scale(stream_key, shape, cuts, -0.22, 0.18) * values
    return jnp.clip(values, min=-limit, max=limit).astype(held_as)


def setup_inputs(seed: int = 0, part: int = 0) -> dict:
    splits = jax.random.split(jax.random.key(seed), 11)
    own_keys = jax.random.split(jax.random.fold_in(splits[10], part), 11)
    return {
        "tokens": centred(own_keys[0], (SLABS, TOK_DEV, D), 1.0, 6.0, ((0, 4), (2, 4))),
        "in_sign": with_ends(jax.random.randint(splits[1], (D,), 0, 2), jax.random.fold_in(splits[1], 1), 0, 1).astype(jnp.int32),
        "qkv_codes": with_ends(jax.random.randint(splits[2], (D // 8, 3, HEADS * HD), 0, 65536), jax.random.fold_in(splits[2], 1), 0, 65535).astype(jnp.int32),
        "qkv_scale": jnp.clip(jnp.exp(math.log(3.0) - 2.3025851 * jax.random.uniform(splits[3], (3, HEADS * HD), jnp.float32) ** block_scale(splits[3], (3, HEADS * HD), ((1, 4),), -0.2, 0.2)), 0.3, 3.0),
        "qkv_sign": with_ends(jax.random.randint(splits[4], (3, HEADS * HD), 0, 2), jax.random.fold_in(splits[4], 1), 0, 1).astype(jnp.int32),
        "windows": draw_windows(jax.random.fold_in(jax.random.fold_in(splits[10], part), 71), part),
        "oin_sign": with_ends(jax.random.randint(splits[6], (HEADS * HD,), 0, 2), jax.random.fold_in(splits[6], 1), 0, 1).astype(jnp.int32),
        "out_codes": with_ends(jax.random.randint(splits[7], (HEADS * HD // 8, D), 0, 65536), jax.random.fold_in(splits[7], 1), 0, 65535).astype(jnp.int32),
        "out_scale": jnp.clip(jnp.exp(jax.random.uniform(splits[8], (D,), jnp.float32, math.log(2.0), math.log(20.0))), 2.0, 20.0),
        "out_sign": with_ends(jax.random.randint(splits[9], (D,), 0, 2), jax.random.fold_in(splits[9], 1), 0, 1).astype(jnp.int32),
    }


epsilon = 1e-06

def sylvester(order_size):
    matrix_now = np.ones((1, 1), np.float32)
    seed_pair = np.array([[1.0, 1.0], [1.0, -1.0]], np.float32)
    while matrix_now.shape[0] < order_size:
        matrix_now = np.kron(matrix_now, seed_pair)
    return matrix_now

def signed(sign_bits):
    return (2 * sign_bits - 1).astype(jnp.float32)

def unpack(packed):
    powers = np.array([4 ** k for k in range(8)], np.int32)
    powers = jnp.asarray(powers.reshape((1, 8) + (1,) * (packed.ndim - 1)), jnp.int32)
    digits = packed[:, None] // powers % 4
    return digits.reshape((packed.shape[0] * 8,) + packed.shape[1:])

def levels(packed, column_scale, fan_in):
    return ((unpack(packed).astype(jnp.float32) - 1.5) * (column_scale * fan_in ** (-0.5))).astype(jnp.bfloat16)

def rotate_exact(matrix_in):
    row_count, columns = matrix_in.shape
    hadamard = jnp.asarray(sylvester(HAD), jnp.float32)
    grouped = matrix_in.astype(jnp.float32).reshape(row_count, columns // HAD, HAD)
    turned = jnp.einsum('rbi,ij->rbj', grouped, hadamard, precision=lax.Precision.HIGHEST)
    return turned.reshape(row_count, columns) * HAD ** (-0.5)

def normalize(vectors):
    return vectors / jnp.sqrt(lax.optimization_barrier(jnp.mean(vectors * vectors, axis=-1, keepdims=True)) + epsilon)

def reference(tokens, in_sign, qkv_codes, qkv_scale, qkv_sign, windows, oin_sign, out_codes, out_scale, out_sign):
    flat_tokens = tokens.reshape(TOKENS, D)
    turned = rotate_exact(flat_tokens.astype(jnp.float32) * signed(in_sign)).astype(jnp.bfloat16)
    qkv_weight = levels(qkv_codes, qkv_scale, D).reshape(D, 3 * HEADS * HD)
    projected = jnp.dot(turned, qkv_weight, preferred_element_type=jnp.float32)
    mixed = rotate_exact(projected) * signed(qkv_sign).reshape(-1)
    mixed = mixed.reshape(TOKENS, 3, HEADS, HD)
    queries = normalize(mixed[:, 0]).astype(jnp.bfloat16).reshape(SLABS, TOK_DEV, HEADS, HD)
    key_rows = normalize(mixed[:, 1]).astype(jnp.bfloat16).reshape(SLABS, TOK_DEV, HEADS, HD)
    value_rows = mixed[:, 2].astype(jnp.bfloat16).reshape(SLABS, TOK_DEV, HEADS, HD)
    padding = jnp.zeros((5, TOK_DEV, HEADS, HD), jnp.bfloat16)
    keys_padded = jnp.concatenate([padding, key_rows, padding], 0)
    values_padded = jnp.concatenate([padding, value_rows, padding], 0)
    local_tiles = jnp.arange(11 * QTILES, dtype=jnp.int32)

    def attend(tile_row):
        near_keys = lax.dynamic_slice_in_dim(keys_padded, tile_row, 11, 0).reshape(11 * TOK_DEV, HEADS, HD)
        near_values = lax.dynamic_slice_in_dim(values_padded, tile_row, 11, 0).reshape(11 * TOK_DEV, HEADS, HD)
        key_ids = (tile_row - 5) * QTILES + local_tiles
        listed = lax.dynamic_index_in_dim(windows, tile_row, 0, keepdims=False)
        allowed = jnp.any(listed[:, :, None] == key_ids[None, None, :], axis=1)
        allowed = jnp.broadcast_to(allowed[:, None, :, None], (QTILES, TILE, 11 * QTILES, TILE))
        allowed = allowed.reshape(TOK_DEV, 11 * TOK_DEV)
        own_queries = lax.dynamic_index_in_dim(queries, tile_row, 0, keepdims=False)
        score = jnp.einsum('qhd,khd->hqk', own_queries.astype(jnp.float32), near_keys.astype(jnp.float32)) * HD ** (-0.5)
        weight = jnp.where(allowed[None], jnp.exp(score), 0.0)
        totals = lax.optimization_barrier(jnp.sum(weight, axis=-1))
        rounded = lax.optimization_barrier(weight.astype(jnp.bfloat16)).astype(jnp.float32)
        gathered_sum = jnp.einsum('hqk,khd->qhd', rounded, near_values.astype(jnp.float32))
        return (gathered_sum / totals.T[:, :, None]).astype(jnp.bfloat16)
    attended = lax.map(attend, jnp.arange(SLABS, dtype=jnp.int32))
    attended = attended.reshape(TOKENS, HEADS * HD)
    rotated_heads = rotate_exact(attended.astype(jnp.float32) * signed(oin_sign)).astype(jnp.bfloat16)
    out_weight = levels(out_codes, out_scale, HEADS * HD)
    group_cols = HEADS * HD // N_HEAD
    summed = jnp.zeros((TOKENS, D), jnp.float32)
    for group in range(N_HEAD):
        group_term = jnp.dot(rotated_heads[:, group * group_cols:(group + 1) * group_cols], out_weight[group * group_cols:(group + 1) * group_cols], preferred_element_type=jnp.float32)
        summed = summed + lax.optimization_barrier(group_term.astype(jnp.bfloat16)).astype(jnp.float32)
    result_rows = (rotate_exact(summed) * signed(out_sign)).astype(jnp.bfloat16)
    return result_rows.reshape(SLABS, TOK_DEV, D)
```

```python
import functools

import jax
import jax.numpy as jnp
import numpy as np
from jax import lax
from jax.experimental import pallas as pl
from jax.experimental.pallas import tpu as pltpu
from jax.sharding import PartitionSpec as P

HD = 128
HAD = 128
TILE = 64
HROWS = 4
PLANES = 8
GROUP = HAD // PLANES
EPSILON = 1e-06
MESH = pl.DeviceIdType.MESH
VLIMIT = 60 * 1024 * 1024


def sylvester(order_size):
    matrix_now = np.ones((1, 1), np.float32)
    seed_pair = np.array([[1.0, 1.0], [1.0, -1.0]], np.float32)
    while matrix_now.shape[0] < order_size:
        matrix_now = np.kron(matrix_now, seed_pair)
    return matrix_now


ORDER = np.array([8 * i + k for k in range(PLANES) for i in range(GROUP)])
PLANE_POWER = np.array([4.0**k for k in range(PLANES) for _ in range(GROUP)], np.float32)


def plain_matrix():
    return jnp.asarray(sylvester(HAD), jnp.bfloat16)


def plane_matrix():
    return jnp.asarray(sylvester(HAD)[:, ORDER], jnp.bfloat16)


def plane_scale():
    return jnp.asarray((HAD**-0.5 / PLANE_POWER)[None, :], jnp.float32)


def plane_power():
    return jnp.asarray(PLANE_POWER[None, :], jnp.float32)


def power_matrix():
    return jnp.asarray(np.repeat(PLANE_POWER[:, None], HAD, axis=1), jnp.bfloat16)


def signed(sign_bits):
    return (2 * sign_bits - 1).astype(jnp.float32)


def dot(left, right):
    return jnp.dot(left, right, preferred_element_type=jnp.float32)


def rotate_split(block, matrix):
    high = block.astype(jnp.bfloat16)
    low = (block - high.astype(jnp.float32)).astype(jnp.bfloat16)
    return (dot(high, matrix) + dot(low, matrix)) * HAD**-0.5


def unpack_block(words):
    planes = [(words & (3 << (2 * k))).astype(jnp.float32).astype(jnp.bfloat16) for k in range(PLANES)]
    pieces = []
    for block in range(words.shape[0] // GROUP):
        for k in range(PLANES):
            pieces.append(planes[k][block * GROUP : (block + 1) * GROUP])
    return jnp.concatenate(pieces, axis=0)


def row_sums(rows, power):
    total = None
    for block in range(rows.shape[1] // HAD):
        part = rows[:, block * HAD : (block + 1) * HAD].astype(jnp.float32) * power
        total = part if total is None else total + part
    return jnp.sum(total, axis=1, keepdims=True)


def layer_kernel(
    n, peers, distances, cols, gcols,
    x_ref, insigns_ref, qscale_ref, qsign_ref, listed_ref, osign_ref, oscale_ref, outsign_ref,
    plane_mat_ref, mat_ref, pscale_ref, power_ref, codes_ref, ocodes_ref,
    out_ref,
    turned, words, weights, acc, offset, qkv, near, owords, oweights, gathered, totals,
    rotated, ooffset, lines, insigns, part, word_sem, oword_sem, halo_send, halo_recv, *scratch,
):
    me = lax.axis_index("head")
    row = lax.axis_index("height")
    rows, width = x_ref.shape
    count = words.shape[0]
    per_part = count // 3
    per_chunk = cols // HD
    local = per_part * cols
    depth = width // PLANES
    qtiles = rows // TILE
    groups = part.shape[0]
    share = rows // n
    slots = len(distances)

    def fetch(j):
        return pltpu.make_async_copy(
            codes_ref.at[(j // per_part + 1) % 3, :, pl.ds(pl.multiple_of(j % per_part * cols, HD), cols)],
            words.at[j],
            word_sem.at[j],
        )

    for j in range(count):
        fetch(j).start()
    fetch_out = pltpu.make_async_copy(ocodes_ref, owords, oword_sem)
    fetch_out.start()

    barrier = pltpu.get_barrier_semaphore()
    if n == 4:
        partner = me + 1 - 2 * (me % 2)
        across = (me + 2) % 4
        diagonal = (partner + 2) % 4
        head_peers = [partner, across]
        early, late = [me, partner], [across, diagonal]
    else:
        head_peers = [(me + p) % n for p in range(1, n)]
        early, late = [me], head_peers
    gives = [jnp.logical_and(row + d >= 0, row + d < peers) for d in distances]
    takes = [jnp.logical_and(row - d >= 0, row - d < peers) for d in distances]
    for peer in head_peers:
        pl.semaphore_signal(barrier, inc=1, device_id={"head": peer}, device_id_type=MESH)
    greeted = jnp.int32(len(head_peers))
    for slot, distance in enumerate(distances):

        @pl.when(gives[slot])
        def _():
            pl.semaphore_signal(
                barrier, inc=1, device_id={"height": row + distance}, device_id_type=MESH
            )

        greeted = greeted + jnp.where(gives[slot], 1, 0)

    for shard in range(n):
        for block in range(width // HAD):
            lanes = slice(block * HAD, (block + 1) * HAD)
            line = signed(insigns_ref[shard * width + block * HAD : shard * width + (block + 1) * HAD])
            insigns[shard, :, lanes] = jnp.broadcast_to(line[None, :], (8, HAD))
    for block in range(width // HAD):
        lanes = slice(block * HAD, (block + 1) * HAD)
        spun = dot(x_ref[:, lanes] * insigns[me, 0:1, lanes].astype(jnp.bfloat16), plane_mat_ref[...])
        turned[me, :, lanes] = (spun * pscale_ref[...]).astype(jnp.bfloat16)
    for j in range(count):
        source = (j // per_part + 1) % 3
        spots = slice(j % per_part * cols, (j % per_part + 1) * cols)
        scale = qscale_ref[source : source + 1, spots] * (width * n) ** -0.5
        sign = signed(qsign_ref[source : source + 1, spots])
        lines[j, 0:8, :] = jnp.broadcast_to(scale, (8, cols))
        lines[j, 8:16, :] = jnp.broadcast_to(sign, (8, cols))
    pl.semaphore_wait(barrier, greeted)

    def head_copy(src, dst, send, recv, peer):
        return pltpu.make_async_remote_copy(
            src, dst, send, recv, device_id={"head": peer}, device_id_type=MESH
        )

    def unpack(j):
        fetch(j).wait()
        for shard in range(n):
            weights[j, shard] = unpack_block(words[j, shard * depth : (shard + 1) * depth, :])
        total = dot(turned[early[0]], weights[j, early[0]])
        for shard in early[1:]:
            total = total + dot(turned[shard], weights[j, shard])
        acc[j] = total

    if n == 4:
        a_send, a_recv, f_send, f_recv, b_send, b_recv = scratch[:6]
        scratch = scratch[6:]
        chunks = a_send.shape[0]
        step = rows // chunks

        def piece(slot, c):
            return turned.at[slot, pl.ds(c * step, step), :]

        crossing = [
            head_copy(piece(me, c), piece(me, c), a_send.at[c], a_recv.at[c], across)
            for c in range(chunks)
        ]
        relays = [
            head_copy(piece(across, c), piece(across, c), f_send.at[c], f_recv.at[c], partner)
            for c in range(chunks)
        ]
        for copy in crossing:
            copy.start()
        beside = head_copy(turned.at[me], turned.at[me], b_send, b_recv, partner)
        beside.start()
        beside.wait_recv()
        done = 0
        for c in range(chunks):
            upto = count * (c + 1) // chunks

            @pl.loop(done, upto)
            def _(j):
                unpack(j)

            done = upto
            crossing[c].wait_recv()
            relays[c].start()
        for copy in relays:
            copy.wait_recv()
        sent = crossing + relays + [beside]
    else:
        g_send, g_recv = scratch[:2]
        scratch = scratch[2:]
        sent = [
            head_copy(turned.at[me], turned.at[me], g_send.at[p], g_recv.at[p], peer)
            for p, peer in enumerate(head_peers)
        ]
        for copy in sent:
            copy.start()

        @pl.loop(0, count)
        def _(j):
            unpack(j)

        for copy in sent:
            copy.wait_recv()

    total = jnp.zeros((rows, 1), jnp.float32)
    for shard in range(n):
        total = total + row_sums(turned[shard], power_ref[...])
    offset[...] = jnp.broadcast_to(1.5 * total, offset.shape)

    def finish(j):
        result = acc[j]
        for shard in late:
            result = result + dot(turned[shard], weights[j, shard])
        source = (j // per_part + 1) % 3
        for head in range(per_chunk):
            lanes = slice(head * HD, (head + 1) * HD)
            block = (result[:, lanes] - offset[...]) * lines[j, 0:1, lanes]
            block = rotate_split(block, mat_ref[...]) * lines[j, 8:9, lanes]
            mean = jnp.mean(block * block, axis=-1, keepdims=True)
            divisor = jnp.where(source < 2, jnp.sqrt(mean + EPSILON), 1.0)
            qkv[j, :, lanes] = (block / divisor).astype(jnp.bfloat16)

    def halo_copy(slot, j):
        return pltpu.make_async_remote_copy(
            qkv.at[j], near.at[slot, j], halo_send.at[slot, j], halo_recv.at[slot, j],
            device_id={"height": row + distances[slot]}, device_id_type=MESH,
        )

    @pl.loop(0, 2 * per_part)
    def _(j):
        finish(j)
        for slot in range(slots):

            @pl.when(gives[slot])
            def _():
                halo_copy(slot, j).start()

    for slot in range(slots):

        @pl.when(jnp.logical_not(takes[slot]))
        def _():
            near[slot] = jnp.zeros(near.shape[1:], near.dtype)

    @pl.loop(2 * per_part, count)
    def _(j):
        finish(j)

    def mask_of(first_tile):
        ids = lax.broadcasted_iota(jnp.int32, (8, rows), 1) // TILE + first_tile
        stack = []
        for tile in range(qtiles):
            hit = ids == listed_ref[tile, 0, 0]
            for entry in range(1, listed_ref.shape[2]):
                hit = jnp.logical_or(hit, ids == listed_ref[tile, 0, entry])
            stack.extend([jnp.where(hit, 1.0, 0.0)] * (TILE // 8))
        return jnp.concatenate(stack, axis=0)

    def attend(queries, keys, values, mask):
        score = lax.dot_general(
            queries, keys, (((1,), (1,)), ((), ())), preferred_element_type=jnp.float32
        )
        weight = jnp.exp(score * HD**-0.5) * mask
        return dot(weight.astype(jnp.bfloat16), values), jnp.sum(weight, axis=-1, keepdims=True)

    own_mask = mask_of(row * qtiles)
    near_masks = [mask_of((row - d) * qtiles) for d in distances]
    for head in range(local // HD):
        chunk, lanes = head // per_chunk, slice(head % per_chunk * HD, (head % per_chunk + 1) * HD)
        found, sums = attend(
            qkv[2 * per_part + chunk, :, lanes], qkv[chunk, :, lanes],
            qkv[per_part + chunk, :, lanes], own_mask,
        )
        gathered[head] = found
        totals[head] = jnp.broadcast_to(sums, found.shape)

    fetch_out.wait()

    @pl.loop(0, groups)
    def _(g):
        spots = pl.ds(pl.multiple_of(g * gcols, HD), gcols)
        oweights[g] = unpack_block(owords[:, spots])

    for head in range(local // HD):
        chunk, lanes = head // per_chunk, slice(head % per_chunk * HD, (head % per_chunk + 1) * HD)
        if head % per_chunk == 0:
            for slot in range(slots):

                @pl.when(takes[slot])
                def _():
                    halo_copy(slot, chunk).wait_recv()
                    halo_copy(slot, per_part + chunk).wait_recv()

        found, sums = gathered[head], totals[head]
        for slot in range(slots):
            more, more_sums = attend(
                qkv[2 * per_part + chunk, :, lanes], near[slot, chunk, :, lanes],
                near[slot, per_part + chunk, :, lanes], near_masks[slot],
            )
            found, sums = found + more, sums + more_sums
        attended = (found / sums).astype(jnp.bfloat16)
        spots = slice(head * HD, (head + 1) * HD)
        spun = dot(attended * signed(osign_ref[spots])[None, :].astype(jnp.bfloat16), plane_mat_ref[...])
        rotated[:, spots] = (spun * pscale_ref[...]).astype(jnp.bfloat16)
    ooffset[...] = jnp.broadcast_to(1.5 * row_sums(rotated[...], power_ref[...]), ooffset.shape)

    def produce(g):
        result = dot(rotated[...], oweights[g])
        for block in range(gcols // HAD):
            lanes = slice(block * HAD, (block + 1) * HAD)
            spots = slice(g * gcols + block * HAD, g * gcols + (block + 1) * HAD)
            value = (result[:, lanes] - ooffset[...]) * (oscale_ref[spots] * (local * n) ** -0.5)[None, :]
            part[g, :, :, lanes] = value.reshape(n, share, HAD).astype(jnp.bfloat16)

    def conclude(g, terms):
        for block in range(gcols // HAD):
            lanes = slice(block * HAD, (block + 1) * HAD)
            spots = slice(g * gcols + block * HAD, g * gcols + (block + 1) * HAD)
            total = part[g, me, :, lanes].astype(jnp.float32)
            for term in terms:
                total = total + term[:, lanes].astype(jnp.float32)
            spun = rotate_split(total, mat_ref[...]) * signed(outsign_ref[spots])[None, :]
            out_ref[:, spots] = spun.astype(jnp.bfloat16)

    if n == 4:
        staged, flank, summed, crossed, p_send, p_recv, q_send, q_recv, x_send, x_recv = scratch
        first = [
            head_copy(part.at[g, diagonal], staged.at[g], p_send.at[g], p_recv.at[g], partner)
            for g in range(groups)
        ]
        second = [
            head_copy(part.at[g, partner], flank.at[g], q_send.at[g], q_recv.at[g], partner)
            for g in range(groups)
        ]
        third = [
            head_copy(summed.at[g], crossed.at[g], x_send.at[g], x_recv.at[g], across)
            for g in range(groups)
        ]

        def relay(g):
            first[g].wait_recv()
            summed[g] = (
                part[g, across].astype(jnp.float32) + staged[g].astype(jnp.float32)
            ).astype(jnp.bfloat16)
            third[g].start()

        for g in range(groups):
            produce(g)
            first[g].start()
            second[g].start()
            if g > 0:
                relay(g - 1)
        relay(groups - 1)
        for g in range(groups):
            second[g].wait_recv()
            third[g].wait_recv()
            conclude(g, [flank[g], crossed[g]])
        sent = sent + first + second + third
    else:
        landed, r_send, r_recv = scratch
        moves = []
        for g in range(groups):
            produce(g)
            move = [
                head_copy(part.at[g, peer], landed.at[p, g], r_send.at[p, g], r_recv.at[p, g], peer)
                for p, peer in enumerate(head_peers)
            ]
            for copy in move:
                copy.start()
            moves.append(move)
        for g in range(groups):
            for copy in moves[g]:
                copy.wait_recv()
            conclude(g, [landed[p, g] for p in range(n - 1)])
        sent = sent + [copy for move in moves for copy in move]

    for copy in sent:
        copy.wait_send()
    for slot in range(slots):

        @pl.when(gives[slot])
        def _():
            for j in range(2 * per_part):
                halo_copy(slot, j).wait_send()


def quad_kernel(
    peers,
    x_ref, insigns_ref, qscale_ref, qsign_ref, listed_ref, osign_ref, oscale_ref, outsign_ref,
    plane_mat_ref, mat_ref, pscale_ref, pmat_ref, codes_ref, ocodes_ref,
    out_ref,
    early_x, late_x, words, early_w, late_w, acc, eoff, offs, pm, lines, insigns, kv, queries, near,
    owords, oweights, num, tot, own_mask, near_mask, rotated, ooff, part, staged, summed, flank, crossed,
    word_sem, oword_sem, a_send, a_recv, f_send, f_recv, b_send, b_recv, halo_send, halo_recv,
    p_send, p_recv, r_send, r_recv, q_send, q_recv, x_send, x_recv,
):
    me = lax.axis_index("head")
    row = lax.axis_index("height")
    rows, width = x_ref.shape
    count, _, cols = words.shape
    per_part = count // 3
    per_chunk = cols // HD
    local = per_part * cols
    depth = width // PLANES
    groups, gcols = part.shape[0], part.shape[3]
    steps = rows // TILE
    unit = part.shape[2]
    heads = local // HD
    chip, core = me // 2, me % 2
    partner = me + 1 - 2 * core
    across = (me + 2) % 4
    diagonal = (partner + 2) % 4
    distances = (1, -1)

    def tile_at(step):
        return chip * step + (1 - chip) * (steps - 1 - step)

    def fetch(j):
        return pltpu.make_async_copy(
            codes_ref.at[(j // per_part + 1) % 3, :, pl.ds(pl.multiple_of(j % per_part * cols, HD), cols)],
            words.at[j],
            word_sem.at[j],
        )

    for j in range(count):
        fetch(j).start()
    fetch_out = pltpu.make_async_copy(ocodes_ref, owords, oword_sem)
    fetch_out.start()

    barrier = pltpu.get_barrier_semaphore()
    gives = [jnp.logical_and(row + d >= 0, row + d < peers) for d in distances]
    takes = [jnp.logical_and(row - d >= 0, row - d < peers) for d in distances]
    for peer in (partner, across, diagonal):
        pl.semaphore_signal(barrier, inc=1, device_id={"head": peer}, device_id_type=MESH)
    greeted = jnp.int32(3)
    for slot, distance in enumerate(distances):

        @pl.when(gives[slot])
        def _():
            pl.semaphore_signal(
                barrier, inc=1, device_id={"height": row + distance}, device_id_type=MESH
            )

        greeted = greeted + jnp.where(gives[slot], 1, 0)

    for shard in range(4):
        for block in range(width // HAD):
            lanes = slice(block * HAD, (block + 1) * HAD)
            line = signed(insigns_ref[shard * width + block * HAD : shard * width + (block + 1) * HAD])
            insigns[shard, :, lanes] = jnp.broadcast_to(line[None, :], (8, HAD))
    for step in reversed(range(steps)):
        start = pl.multiple_of(tile_at(step) * TILE, TILE)
        for block in range(width // HAD):
            lanes = slice(block * HAD, (block + 1) * HAD)
            plain = x_ref[pl.ds(start, TILE), lanes] * insigns[me, 0:1, lanes].astype(jnp.bfloat16)
            spun = dot(plain, plane_mat_ref[...])
            early_x[0, step, :, lanes] = (spun * pscale_ref[...]).astype(jnp.bfloat16)

    def head_copy(src, dst, send, recv, peer):
        return pltpu.make_async_remote_copy(
            src, dst, send, recv, device_id={"head": peer}, device_id_type=MESH
        )

    crossing = [
        head_copy(early_x.at[0, steps - 1 - i], late_x.at[0, i], a_send.at[i], a_recv.at[i], across)
        for i in range(steps)
    ]
    relays = [
        head_copy(late_x.at[0, i], late_x.at[1, i], f_send.at[i], f_recv.at[i], partner)
        for i in range(steps)
    ]
    beside = head_copy(early_x.at[0], early_x.at[1], b_send, b_recv, partner)
    pl.semaphore_wait(barrier, greeted)
    for copy in crossing:
        copy.start()
    beside.start()

    for block in range(width // HAD):
        pm[block * HAD : (block + 1) * HAD, :] = pmat_ref[...]
    for j in range(count):
        source = (j // per_part + 1) % 3
        spots = slice(j % per_part * cols, (j % per_part + 1) * cols)
        scale = qscale_ref[source : source + 1, spots] * (width * 4) ** -0.5
        sign = signed(qsign_ref[source : source + 1, spots]) * HAD**-0.5
        lines[j, 0:8, :] = jnp.broadcast_to(scale, (8, cols))
        lines[j, 8:16, :] = jnp.broadcast_to(sign, (8, cols))
    for slot in range(2):

        @pl.when(jnp.logical_not(takes[slot]))
        def _():
            near[slot] = jnp.zeros(near.shape[1:], near.dtype)

    def listed_mask(step, ids):
        tile = tile_at(step)
        hit = ids == listed_ref[tile, 0, 0]
        for entry in range(1, listed_ref.shape[2]):
            hit = jnp.logical_or(hit, ids == listed_ref[tile, 0, entry])
        return jnp.where(hit, 1.0, 0.0)

    own_ids = tile_at(lax.broadcasted_iota(jnp.int32, (8, rows), 1) // TILE) + row * steps
    for step in range(steps):
        own_mask[step] = listed_mask(step, own_ids)
    side = lax.broadcasted_iota(jnp.int32, (8, 2 * TILE), 1) // TILE
    side_row = row - 1 + 2 * side
    for s in range(steps):
        for step in range(steps):
            if abs(s - step) < 2:
                near_mask[s, step] = listed_mask(step, side_row * steps + tile_at(s))

    shards = [me, partner, across, diagonal]

    def unpack_role(j, role, target):
        for block in range(depth // GROUP):
            start = pl.multiple_of(shards[role] * depth + block * GROUP, GROUP)
            block_words = words[j, pl.ds(start, GROUP), :]
            for k in range(PLANES):
                spot = block * HAD + k * GROUP
                plane = (block_words & (3 << (2 * k))).astype(jnp.float32).astype(jnp.bfloat16)
                target[role % 2, spot : spot + GROUP, :] = plane

    def prepare(j):
        fetch(j).wait()
        for role in range(2):
            unpack_role(j, role, early_w)
        total = dot(early_x[0].reshape(rows, width), early_w[0])
        total = total + dot(early_x[1].reshape(rows, width), early_w[1])
        for role in range(2, 4):
            unpack_role(j, role, late_w.at[j])
        acc[j] = total.reshape(steps, TILE, cols)

    beside.wait_recv()
    total = dot(early_x[0].reshape(rows, width), pm[...])
    total = total + dot(early_x[1].reshape(rows, width), pm[...])
    eoff[...] = total.reshape(steps, TILE, HD)

    def spread(c):
        spots = pl.ds(pl.multiple_of(c * gcols, HD), gcols)
        for block in range(owords.shape[0] // GROUP):
            block_words = owords[block * GROUP : (block + 1) * GROUP, spots]
            for k in range(PLANES):
                spot = block * HAD + k * GROUP
                plane = (block_words & (3 << (2 * k))).astype(jnp.float32).astype(jnp.bfloat16)
                oweights[c, spot : spot + GROUP, :] = plane

    def halo_copy(slot, step, c):
        return pltpu.make_async_remote_copy(
            kv.at[step, c], near.at[slot, step, c],
            halo_send.at[slot, step, c], halo_recv.at[slot, step, c],
            device_id={"height": row + distances[slot]}, device_id_type=MESH,
        )

    def project(step):
        late = dot(late_x[0, step], pm[...]) + dot(late_x[1, step], pm[...])
        offs[...] = 1.5 * (eoff[step] + late)

        @pl.loop(0, per_part)
        def _(c):
            for kind in range(3):
                j = kind * per_part + c
                result = acc[j, step] + dot(late_x[0, step], late_w[j, 0])
                result = result + dot(late_x[1, step], late_w[j, 1])
                stack, factors = [], []
                for head in range(per_chunk):
                    lanes = slice(head * HD, (head + 1) * HD)
                    block = (result[:, lanes] - offs[...]) * lines[j, 0:1, lanes]
                    high = block.astype(jnp.bfloat16)
                    stack += [high, (block - high.astype(jnp.float32)).astype(jnp.bfloat16)]
                    if kind != 1:
                        mean = jnp.mean(block * block, axis=-1, keepdims=True)
                        factors.append(lax.rsqrt(mean + EPSILON))
                spun = dot(jnp.concatenate(stack, axis=0), mat_ref[...])
                for head in range(per_chunk):
                    lanes = slice(head * HD, (head + 1) * HD)
                    at = 2 * head * TILE
                    value = (spun[at : at + TILE] + spun[at + TILE : at + 2 * TILE]) * lines[j, 8:9, lanes]
                    if kind != 1:
                        value = value * factors[head]
                    if kind == 2:
                        queries[step, c, :, lanes] = value.astype(jnp.bfloat16)
                    else:
                        kv[step, c, kind, :, lanes] = value.astype(jnp.bfloat16)
            for slot in range(2):

                @pl.when(gives[slot])
                def _():
                    halo_copy(slot, step, c).start()

    @pl.loop(0, count - 2)
    def _(j):
        prepare(j)

    crossing[0].wait_recv()
    relays[0].start()

    @pl.loop(count - 2, count)
    def _(j):
        prepare(j)

    relays[0].wait_recv()
    project(0)
    crossing[1].wait_recv()
    relays[1].start()
    fetch_out.wait()

    @pl.loop(0, 2)
    def _(c):
        spread(c)

    relays[1].wait_recv()
    project(1)
    crossing[2].wait_recv()
    relays[2].start()

    @pl.loop(2, groups)
    def _(c):
        spread(c)

    relays[2].wait_recv()
    project(2)

    def attend(rows_q, keys, values, mask):
        score = lax.dot_general(
            rows_q, keys, (((1,), (1,)), ((), ())), preferred_element_type=jnp.float32
        )
        weight = jnp.exp(score * HD**-0.5) * mask
        return dot(weight.astype(jnp.bfloat16), values), jnp.sum(weight, axis=-1, keepdims=True)

    def lanes_of(head):
        return slice(head % per_chunk * HD, (head % per_chunk + 1) * HD)

    def broad(masks):
        return jnp.concatenate([jnp.broadcast_to(m[0:1], (TILE, m.shape[1])) for m in masks], axis=0)

    everything = range(steps)
    mask = broad([own_mask[a] for a in everything])
    for head in range(heads):
        c, lanes = head // per_chunk, lanes_of(head)
        found, sums = attend(
            jnp.concatenate([queries[a, c, :, lanes] for a in everything], axis=0),
            jnp.concatenate([kv[a, c, 0, :, lanes] for a in everything], axis=0),
            jnp.concatenate([kv[a, c, 1, :, lanes] for a in everything], axis=0),
            mask,
        )
        num[:, head] = found.reshape(steps, TILE, HD)
        tot[:, head] = jnp.broadcast_to(sums, found.shape).reshape(steps, TILE, HD)

    def near_wait(s):
        for slot in range(2):

            @pl.when(takes[slot])
            def _():
                for c in range(per_part):
                    halo_copy(slot, s, c).wait_recv()

    def near_attend(s, over):
        mask = broad([near_mask[s, a] for a in over])
        for head in range(heads):
            c, lanes = head // per_chunk, lanes_of(head)
            found, sums = attend(
                jnp.concatenate([queries[a, c, :, lanes] for a in over], axis=0),
                jnp.concatenate([near[slot, s, c, 0, :, lanes] for slot in range(2)], axis=0),
                jnp.concatenate([near[slot, s, c, 1, :, lanes] for slot in range(2)], axis=0),
                mask,
            )
            for at, a in enumerate(over):
                span = slice(at * TILE, (at + 1) * TILE)
                num[a, head] = num[a, head] + found[span]
                tot[a, head] = tot[a, head] + sums[span]

    def complete(over):
        for head in range(heads):
            spots = slice(head * HD, (head + 1) * HD)
            attended = jnp.concatenate([num[a, head] / tot[a, head] for a in over], axis=0)
            attended = attended.astype(jnp.bfloat16) * signed(osign_ref[spots])[None, :].astype(jnp.bfloat16)
            spun = (dot(attended, plane_mat_ref[...]) * pscale_ref[...]).astype(jnp.bfloat16)
            for at, a in enumerate(over):
                rotated[a, :, spots] = spun[at * TILE : (at + 1) * TILE]
        for a in over:
            ooff[a] = 1.5 * dot(rotated[a], pm[0:local, :])

    def produce(g, over):
        left = jnp.concatenate([rotated[a] for a in over], axis=0)
        shift = jnp.concatenate([ooff[a] for a in over], axis=0)
        result = dot(left, oweights[g])
        for block in range(gcols // HAD):
            lanes = slice(block * HAD, (block + 1) * HAD)
            spots = slice(g * gcols + block * HAD, g * gcols + (block + 1) * HAD)
            value = (result[:, lanes] - shift) * (oscale_ref[spots] * (local * 4) ** -0.5)[None, :]
            value = value.astype(jnp.bfloat16)
            for at, a in enumerate(over):
                piece = value[at * TILE : (at + 1) * TILE].reshape(TILE // unit, unit, HAD)
                part[g, pl.ds(tile_at(a) * (TILE // unit), TILE // unit), :, lanes] = piece

    first_base = tile_at(0) * (TILE // unit)
    second_base = TILE // unit + (1 - chip) * 2
    own_base = 3 * me

    def cross_copy(g, k, chunk):
        return head_copy(
            summed.at[g, k], crossed.at[g, chunk % 3], x_send.at[g, k], x_recv.at[g, chunk % 3], chunk // 3
        )

    def arrival(g, k):
        return head_copy(summed.at[g, k], crossed.at[g, k], x_send.at[g, k], x_recv.at[g, k], across)

    def add_up(g, k, chunk):
        summed[g, k] = (
            part[g, chunk].astype(jnp.float32) + staged[g, k].astype(jnp.float32)
        ).astype(jnp.bfloat16)
        cross_copy(g, k, chunk).start()

    first = [
        head_copy(
            part.at[g, pl.ds(first_base + 2 * (1 - core), 2)], staged.at[g, pl.ds(0, 2)],
            p_send.at[g], p_recv.at[g], partner,
        )
        for g in range(groups)
    ]
    second = [
        head_copy(
            part.at[g, pl.ds(second_base + 1 - core, 1)], staged.at[g, pl.ds(2, 1)],
            r_send.at[g], r_recv.at[g], partner,
        )
        for g in range(groups)
    ]
    flanks = [
        head_copy(part.at[g, pl.ds(3 * partner, 3)], flank.at[g], q_send.at[g], q_recv.at[g], partner)
        for g in range(groups)
    ]

    def relay_first(g):
        first[g].wait_recv()
        for k in range(2):
            add_up(g, k, first_base + 2 * core + k)

    def relay_second(g):
        second[g].wait_recv()
        add_up(g, 2, second_base + core)

    near_wait(0)
    near_attend(0, (0, 1))
    near_wait(1)
    near_attend(1, (0,))
    complete((0,))
    for g in range(groups):
        produce(g, (0,))
        first[g].start()
        if g > 0:
            relay_first(g - 1)
    relay_first(groups - 1)
    near_attend(1, (1, 2))
    near_wait(2)
    near_attend(2, (1, 2))
    complete((1, 2))
    for g in range(groups):
        produce(g, (1, 2))
        second[g].start()
        flanks[g].start()
        if g > 0:
            relay_second(g - 1)
    relay_second(groups - 1)

    for g in range(groups):
        flanks[g].wait_recv()
        for k in range(3):
            arrival(g, k).wait_recv()
        for block in range(gcols // HAD):
            lanes = slice(block * HAD, (block + 1) * HAD)
            spots = slice(g * gcols + block * HAD, g * gcols + (block + 1) * HAD)
            total = part[g, pl.ds(own_base, 3), :, lanes].astype(jnp.float32)
            total = total + flank[g, :, :, lanes].astype(jnp.float32)
            total = total + crossed[g, :, :, lanes].astype(jnp.float32)
            spun = rotate_split(total.reshape(3 * unit, HAD), mat_ref[...])
            out_ref[:, spots] = (spun * signed(outsign_ref[spots])[None, :]).astype(jnp.bfloat16)

    for copy in crossing + relays + [beside] + first + second + flanks:
        copy.wait_send()
    for g in range(groups):
        for k in range(3):
            arrival(g, k).wait_send()
    for slot in range(2):

        @pl.when(gives[slot])
        def _():
            for step in range(steps):
                for c in range(per_part):
                    halo_copy(slot, step, c).wait_send()


def quad_call(peers, own, in_sign, qkv_codes, qkv_scale, qkv_sign, windows, oin_sign, out_codes, out_scale, out_sign):
    rows, width = own.shape
    local = qkv_scale.shape[1]
    features = out_codes.shape[1]
    cols = 2 * HD
    count = 3 * local // cols
    per_part = count // 3
    inner = qkv_codes.shape[0]
    gcols = 1024
    groups = features // gcols
    steps = rows // TILE
    heads = local // HD
    unit = rows // 12
    dma = pltpu.SemaphoreType.DMA
    bf16, f32 = jnp.bfloat16, jnp.float32
    vmem = pl.BlockSpec(memory_space=pltpu.VMEM)
    anywhere = pl.BlockSpec(memory_space=pl.ANY)
    smem = pl.BlockSpec(memory_space=pltpu.SMEM)
    triple = pltpu.VMEM((groups, 3, unit, gcols), bf16)
    return pl.pallas_call(
        functools.partial(quad_kernel, peers),
        name="layer",
        out_shape=jax.ShapeDtypeStruct((rows // 4, features), bf16),
        in_specs=[vmem] * 4 + [smem] + [vmem] * 7 + [anywhere] * 2,
        out_specs=vmem,
        scratch_shapes=[
            pltpu.VMEM((2, steps, TILE, width), bf16),
            pltpu.VMEM((2, steps, TILE, width), bf16),
            pltpu.VMEM((count, inner, cols), jnp.int32),
            pltpu.VMEM((2, width, cols), bf16),
            pltpu.VMEM((count, 2, width, cols), bf16),
            pltpu.VMEM((count, steps, TILE, cols), f32),
            pltpu.VMEM((steps, TILE, HD), f32),
            pltpu.VMEM((TILE, HD), f32),
            pltpu.VMEM((width, HD), bf16),
            pltpu.VMEM((count, 16, cols), f32),
            pltpu.VMEM((4, 8, width), f32),
            pltpu.VMEM((steps, per_part, 2, TILE, cols), bf16),
            pltpu.VMEM((steps, per_part, TILE, cols), bf16),
            pltpu.VMEM((2, steps, per_part, 2, TILE, cols), bf16),
            pltpu.VMEM(out_codes.shape, jnp.int32),
            pltpu.VMEM((groups, local, gcols), bf16),
            pltpu.VMEM((steps, heads, TILE, HD), f32),
            pltpu.VMEM((steps, heads, TILE, HD), f32),
            pltpu.VMEM((steps, 8, rows), f32),
            pltpu.VMEM((steps, steps, 8, 2 * TILE), f32),
            pltpu.VMEM((steps, TILE, local), bf16),
            pltpu.VMEM((steps, TILE, HD), f32),
            pltpu.VMEM((groups, 12, unit, gcols), bf16),
            triple,
            triple,
            triple,
            triple,
            dma((count,)),
            dma,
            dma((steps,)),
            dma((steps,)),
            dma((steps,)),
            dma((steps,)),
            dma,
            dma,
            dma((2, steps, per_part)),
            dma((2, steps, per_part)),
            dma((groups,)),
            dma((groups,)),
            dma((groups,)),
            dma((groups,)),
            dma((groups,)),
            dma((groups,)),
            dma((groups, 3)),
            dma((groups, 3)),
        ],
        compiler_params=pltpu.CompilerParams(
            collective_id=0, has_side_effects=True, vmem_limit_bytes=VLIMIT
        ),
    )(
        own,
        in_sign,
        qkv_scale,
        qkv_sign,
        jnp.transpose(windows, (1, 0, 2)),
        oin_sign,
        out_scale,
        out_sign,
        plane_matrix(),
        plain_matrix(),
        plane_scale(),
        power_matrix(),
        jnp.transpose(qkv_codes, (1, 0, 2)),
        out_codes,
    )


def on_device(
    n,
    peers,
    tokens,
    in_sign,
    qkv_codes,
    qkv_scale,
    qkv_sign,
    windows,
    oin_sign,
    out_codes,
    out_scale,
    out_sign,
):
    own = tokens[0]
    rows, width = own.shape
    local = qkv_scale.shape[1]
    features = out_codes.shape[1]
    fitting = rows == 3 * TILE and local % (2 * HD) == 0 and features % 1024 == 0
    if n == 4 and peers <= HROWS and fitting:
        return quad_call(
            peers, own, in_sign, qkv_codes, qkv_scale, qkv_sign, windows,
            oin_sign, out_codes, out_scale, out_sign,
        )[None]
    reach = (1,) if peers <= HROWS else (1, HROWS - 1, HROWS, HROWS + 1)
    distances = tuple(d for r in reach if r < peers for d in (r, -r))
    slots = len(distances)
    cols = 256 if local % 256 == 0 else HD
    count = 3 * local // cols
    per_part = count // 3
    inner = qkv_codes.shape[0]
    gcols = 1024 if features % 1024 == 0 else HD
    groups = features // gcols
    share = rows // n
    chunks = 4
    dma = pltpu.SemaphoreType.DMA
    grouped = pltpu.VMEM((groups, share, gcols), jnp.bfloat16)
    if n == 4:
        tail = [dma((chunks,))] * 4 + [dma] * 2 + [grouped] * 4 + [dma((groups,))] * 6
    else:
        tail = [dma((n - 1,))] * 2
        tail += [pltpu.VMEM((n - 1, groups, share, gcols), jnp.bfloat16)]
        tail += [dma((n - 1, groups))] * 2
    vmem = pl.BlockSpec(memory_space=pltpu.VMEM)
    anywhere = pl.BlockSpec(memory_space=pl.ANY)
    smem = pl.BlockSpec(memory_space=pltpu.SMEM)
    result = pl.pallas_call(
        functools.partial(layer_kernel, n, peers, distances, cols, gcols),
        name="layer",
        out_shape=jax.ShapeDtypeStruct((share, features), jnp.bfloat16),
        in_specs=[vmem] * 4 + [smem] + [vmem] * 7 + [anywhere] * 2,
        out_specs=vmem,
        scratch_shapes=[
            pltpu.VMEM((n, rows, width), jnp.bfloat16),
            pltpu.VMEM((count, inner, cols), jnp.int32),
            pltpu.VMEM((count, n, width, cols), jnp.bfloat16),
            pltpu.VMEM((count, rows, cols), jnp.float32),
            pltpu.VMEM((rows, HD), jnp.float32),
            pltpu.VMEM((count, rows, cols), jnp.bfloat16),
            pltpu.VMEM((slots, 2 * per_part, rows, cols), jnp.bfloat16),
            pltpu.VMEM(out_codes.shape, jnp.int32),
            pltpu.VMEM((groups, local, gcols), jnp.bfloat16),
            pltpu.VMEM((local // HD, rows, HD), jnp.float32),
            pltpu.VMEM((local // HD, rows, HD), jnp.float32),
            pltpu.VMEM((rows, local), jnp.bfloat16),
            pltpu.VMEM((rows, HD), jnp.float32),
            pltpu.VMEM((count, 16, cols), jnp.float32),
            pltpu.VMEM((n, 8, width), jnp.float32),
            pltpu.VMEM((groups, n, share, gcols), jnp.bfloat16),
            dma((count,)),
            dma,
            dma((slots, 2 * per_part)),
            dma((slots, 2 * per_part)),
        ]
        + tail,
        compiler_params=pltpu.CompilerParams(
            collective_id=0, has_side_effects=True, vmem_limit_bytes=VLIMIT
        ),
    )(
        own,
        in_sign,
        qkv_scale,
        qkv_sign,
        jnp.transpose(windows, (1, 0, 2)),
        oin_sign,
        out_scale,
        out_sign,
        plane_matrix(),
        plain_matrix(),
        plane_scale(),
        plane_power(),
        jnp.transpose(qkv_codes, (1, 0, 2)),
        out_codes,
    )
    return result[None]


def solution(mesh):
    n = mesh.shape["head"]
    peers = mesh.shape["height"]
    return jax.shard_map(
        functools.partial(on_device, n, peers),
        mesh=mesh,
        in_specs=(
            P(("clip", "height"), None, "head"),
            P(),
            P(None, None, "head"),
            P(None, "head"),
            P(None, "head"),
            P(("clip", "height"), None, None),
            P("head"),
            P("head", None),
            P(),
            P(),
        ),
        out_specs=P(("clip", "height"), "head", None),
        check_vma=False,
    )
```

```python
import functools

import jax
import jax.numpy as jnp
import numpy as np
from jax import lax
from jax.experimental import pallas as pl
from jax.experimental.pallas import tpu as pltpu
from jax.sharding import PartitionSpec as P

HD = 128
HAD = 128
TILE = 64
HROWS = 4
PLANES = 8
GROUP = HAD // PLANES
EPSILON = 1e-06
MESH = pl.DeviceIdType.MESH
VLIMIT = 60 * 1024 * 1024


def sylvester(order_size):
    matrix_now = np.ones((1, 1), np.float32)
    seed_pair = np.array([[1.0, 1.0], [1.0, -1.0]], np.float32)
    while matrix_now.shape[0] < order_size:
        matrix_now = np.kron(matrix_now, seed_pair)
    return matrix_now


ORDER = np.array([8 * i + k for k in range(PLANES) for i in range(GROUP)])
PLANE_POWER = np.array([4.0**k for k in range(PLANES) for _ in range(GROUP)], np.float32)


def plain_matrix():
    return jnp.asarray(sylvester(HAD), jnp.bfloat16)


def plane_matrix():
    return jnp.asarray(sylvester(HAD)[:, ORDER], jnp.bfloat16)


def plane_scale():
    return jnp.asarray((HAD**-0.5 / PLANE_POWER)[None, :], jnp.float32)


def plane_power():
    return jnp.asarray(PLANE_POWER[None, :], jnp.float32)


def power_matrix():
    return jnp.asarray(np.repeat(PLANE_POWER[:, None], HAD, axis=1), jnp.bfloat16)


def signed(sign_bits):
    return (2 * sign_bits - 1).astype(jnp.float32)


def dot(left, right):
    return jnp.dot(left, right, preferred_element_type=jnp.float32)


def rotate_split(block, matrix):
    high = block.astype(jnp.bfloat16)
    low = (block - high.astype(jnp.float32)).astype(jnp.bfloat16)
    return (dot(high, matrix) + dot(low, matrix)) * HAD**-0.5


def unpack_block(words):
    planes = [(words & (3 << (2 * k))).astype(jnp.float32).astype(jnp.bfloat16) for k in range(PLANES)]
    pieces = []
    for block in range(words.shape[0] // GROUP):
        for k in range(PLANES):
            pieces.append(planes[k][block * GROUP : (block + 1) * GROUP])
    return jnp.concatenate(pieces, axis=0)


def row_sums(rows, power):
    total = None
    for block in range(rows.shape[1] // HAD):
        part = rows[:, block * HAD : (block + 1) * HAD].astype(jnp.float32) * power
        total = part if total is None else total + part
    return jnp.sum(total, axis=1, keepdims=True)


def layer_kernel(
    n, peers, distances, cols, gcols,
    x_ref, insigns_ref, qscale_ref, qsign_ref, listed_ref, osign_ref, oscale_ref, outsign_ref,
    plane_mat_ref, mat_ref, pscale_ref, power_ref, codes_ref, ocodes_ref,
    out_ref,
    turned, words, weights, acc, offset, qkv, near, owords, oweights, gathered, totals,
    rotated, ooffset, lines, insigns, part, word_sem, oword_sem, halo_send, halo_recv, *scratch,
):
    me = lax.axis_index("head")
    row = lax.axis_index("height")
    rows, width = x_ref.shape
    count = words.shape[0]
    per_part = count // 3
    per_chunk = cols // HD
    local = per_part * cols
    depth = width // PLANES
    qtiles = rows // TILE
    groups = part.shape[0]
    share = rows // n
    slots = len(distances)

    def fetch(j):
        return pltpu.make_async_copy(
            codes_ref.at[(j // per_part + 1) % 3, :, pl.ds(pl.multiple_of(j % per_part * cols, HD), cols)],
            words.at[j],
            word_sem.at[j],
        )

    for j in range(count):
        fetch(j).start()
    fetch_out = pltpu.make_async_copy(ocodes_ref, owords, oword_sem)
    fetch_out.start()

    barrier = pltpu.get_barrier_semaphore()
    if n == 4:
        partner = me + 1 - 2 * (me % 2)
        across = (me + 2) % 4
        diagonal = (partner + 2) % 4
        head_peers = [partner, across]
        early, late = [me, partner], [across, diagonal]
    else:
        head_peers = [(me + p) % n for p in range(1, n)]
        early, late = [me], head_peers
    gives = [jnp.logical_and(row + d >= 0, row + d < peers) for d in distances]
    takes = [jnp.logical_and(row - d >= 0, row - d < peers) for d in distances]
    for peer in head_peers:
        pl.semaphore_signal(barrier, inc=1, device_id={"head": peer}, device_id_type=MESH)
    greeted = jnp.int32(len(head_peers))
    for slot, distance in enumerate(distances):

        @pl.when(gives[slot])
        def _():
            pl.semaphore_signal(
                barrier, inc=1, device_id={"height": row + distance}, device_id_type=MESH
            )

        greeted = greeted + jnp.where(gives[slot], 1, 0)

    for shard in range(n):
        for block in range(width // HAD):
            lanes = slice(block * HAD, (block + 1) * HAD)
            line = signed(insigns_ref[shard * width + block * HAD : shard * width + (block + 1) * HAD])
            insigns[shard, :, lanes] = jnp.broadcast_to(line[None, :], (8, HAD))
    for block in range(width // HAD):
        lanes = slice(block * HAD, (block + 1) * HAD)
        spun = dot(x_ref[:, lanes] * insigns[me, 0:1, lanes].astype(jnp.bfloat16), plane_mat_ref[...])
        turned[me, :, lanes] = (spun * pscale_ref[...]).astype(jnp.bfloat16)
    for j in range(count):
        source = (j // per_part + 1) % 3
        spots = slice(j % per_part * cols, (j % per_part + 1) * cols)
        scale = qscale_ref[source : source + 1, spots] * (width * n) ** -0.5
        sign = signed(qsign_ref[source : source + 1, spots])
        lines[j, 0:8, :] = jnp.broadcast_to(scale, (8, cols))
        lines[j, 8:16, :] = jnp.broadcast_to(sign, (8, cols))
    pl.semaphore_wait(barrier, greeted)

    def head_copy(src, dst, send, recv, peer):
        return pltpu.make_async_remote_copy(
            src, dst, send, recv, device_id={"head": peer}, device_id_type=MESH
        )

    def unpack(j):
        fetch(j).wait()
        for shard in range(n):
            weights[j, shard] = unpack_block(words[j, shard * depth : (shard + 1) * depth, :])
        total = dot(turned[early[0]], weights[j, early[0]])
        for shard in early[1:]:
            total = total + dot(turned[shard], weights[j, shard])
        acc[j] = total

    if n == 4:
        a_send, a_recv, f_send, f_recv, b_send, b_recv = scratch[:6]
        scratch = scratch[6:]
        chunks = a_send.shape[0]
        step = rows // chunks

        def piece(slot, c):
            return turned.at[slot, pl.ds(c * step, step), :]

        crossing = [
            head_copy(piece(me, c), piece(me, c), a_send.at[c], a_recv.at[c], across)
            for c in range(chunks)
        ]
        relays = [
            head_copy(piece(across, c), piece(across, c), f_send.at[c], f_recv.at[c], partner)
            for c in range(chunks)
        ]
        for copy in crossing:
            copy.start()
        beside = head_copy(turned.at[me], turned.at[me], b_send, b_recv, partner)
        beside.start()
        beside.wait_recv()
        done = 0
        for c in range(chunks):
            upto = count * (c + 1) // chunks

            @pl.loop(done, upto)
            def _(j):
                unpack(j)

            done = upto
            crossing[c].wait_recv()
            relays[c].start()
        for copy in relays:
            copy.wait_recv()
        sent = crossing + relays + [beside]
    else:
        g_send, g_recv = scratch[:2]
        scratch = scratch[2:]
        sent = [
            head_copy(turned.at[me], turned.at[me], g_send.at[p], g_recv.at[p], peer)
            for p, peer in enumerate(head_peers)
        ]
        for copy in sent:
            copy.start()

        @pl.loop(0, count)
        def _(j):
            unpack(j)

        for copy in sent:
            copy.wait_recv()

    total = jnp.zeros((rows, 1), jnp.float32)
    for shard in range(n):
        total = total + row_sums(turned[shard], power_ref[...])
    offset[...] = jnp.broadcast_to(1.5 * total, offset.shape)

    def finish(j):
        result = acc[j]
        for shard in late:
            result = result + dot(turned[shard], weights[j, shard])
        source = (j // per_part + 1) % 3
        for head in range(per_chunk):
            lanes = slice(head * HD, (head + 1) * HD)
            block = (result[:, lanes] - offset[...]) * lines[j, 0:1, lanes]
            block = rotate_split(block, mat_ref[...]) * lines[j, 8:9, lanes]
            mean = jnp.mean(block * block, axis=-1, keepdims=True)
            divisor = jnp.where(source < 2, jnp.sqrt(mean + EPSILON), 1.0)
            qkv[j, :, lanes] = (block / divisor).astype(jnp.bfloat16)

    def halo_copy(slot, j):
        return pltpu.make_async_remote_copy(
            qkv.at[j], near.at[slot, j], halo_send.at[slot, j], halo_recv.at[slot, j],
            device_id={"height": row + distances[slot]}, device_id_type=MESH,
        )

    @pl.loop(0, 2 * per_part)
    def _(j):
        finish(j)
        for slot in range(slots):

            @pl.when(gives[slot])
            def _():
                halo_copy(slot, j).start()

    for slot in range(slots):

        @pl.when(jnp.logical_not(takes[slot]))
        def _():
            near[slot] = jnp.zeros(near.shape[1:], near.dtype)

    @pl.loop(2 * per_part, count)
    def _(j):
        finish(j)

    def mask_of(first_tile):
        ids = lax.broadcasted_iota(jnp.int32, (8, rows), 1) // TILE + first_tile
        stack = []
        for tile in range(qtiles):
            hit = ids == listed_ref[tile, 0, 0]
            for entry in range(1, listed_ref.shape[2]):
                hit = jnp.logical_or(hit, ids == listed_ref[tile, 0, entry])
            stack.extend([jnp.where(hit, 1.0, 0.0)] * (TILE // 8))
        return jnp.concatenate(stack, axis=0)

    def attend(queries, keys, values, mask):
        score = lax.dot_general(
            queries, keys, (((1,), (1,)), ((), ())), preferred_element_type=jnp.float32
        )
        weight = jnp.exp(score * HD**-0.5) * mask
        return dot(weight.astype(jnp.bfloat16), values), jnp.sum(weight, axis=-1, keepdims=True)

    own_mask = mask_of(row * qtiles)
    near_masks = [mask_of((row - d) * qtiles) for d in distances]
    for head in range(local // HD):
        chunk, lanes = head // per_chunk, slice(head % per_chunk * HD, (head % per_chunk + 1) * HD)
        found, sums = attend(
            qkv[2 * per_part + chunk, :, lanes], qkv[chunk, :, lanes],
            qkv[per_part + chunk, :, lanes], own_mask,
        )
        gathered[head] = found
        totals[head] = jnp.broadcast_to(sums, found.shape)

    fetch_out.wait()

    @pl.loop(0, groups)
    def _(g):
        spots = pl.ds(pl.multiple_of(g * gcols, HD), gcols)
        oweights[g] = unpack_block(owords[:, spots])

    for head in range(local // HD):
        chunk, lanes = head // per_chunk, slice(head % per_chunk * HD, (head % per_chunk + 1) * HD)
        if head % per_chunk == 0:
            for slot in range(slots):

                @pl.when(takes[slot])
                def _():
                    halo_copy(slot, chunk).wait_recv()
                    halo_copy(slot, per_part + chunk).wait_recv()

        found, sums = gathered[head], totals[head]
        for slot in range(slots):
            more, more_sums = attend(
                qkv[2 * per_part + chunk, :, lanes], near[slot, chunk, :, lanes],
                near[slot, per_part + chunk, :, lanes], near_masks[slot],
            )
            found, sums = found + more, sums + more_sums
        attended = (found / sums).astype(jnp.bfloat16)
        spots = slice(head * HD, (head + 1) * HD)
        spun = dot(attended * signed(osign_ref[spots])[None, :].astype(jnp.bfloat16), plane_mat_ref[...])
        rotated[:, spots] = (spun * pscale_ref[...]).astype(jnp.bfloat16)
    ooffset[...] = jnp.broadcast_to(1.5 * row_sums(rotated[...], power_ref[...]), ooffset.shape)

    def produce(g):
        result = dot(rotated[...], oweights[g])
        for block in range(gcols // HAD):
            lanes = slice(block * HAD, (block + 1) * HAD)
            spots = slice(g * gcols + block * HAD, g * gcols + (block + 1) * HAD)
            value = (result[:, lanes] - ooffset[...]) * (oscale_ref[spots] * (local * n) ** -0.5)[None, :]
            part[g, :, :, lanes] = value.reshape(n, share, HAD).astype(jnp.bfloat16)

    def conclude(g, terms):
        for block in range(gcols // HAD):
            lanes = slice(block * HAD, (block + 1) * HAD)
            spots = slice(g * gcols + block * HAD, g * gcols + (block + 1) * HAD)
            total = part[g, me, :, lanes].astype(jnp.float32)
            for term in terms:
                total = total + term[:, lanes].astype(jnp.float32)
            spun = rotate_split(total, mat_ref[...]) * signed(outsign_ref[spots])[None, :]
            out_ref[:, spots] = spun.astype(jnp.bfloat16)

    if n == 4:
        staged, flank, summed, crossed, p_send, p_recv, q_send, q_recv, x_send, x_recv = scratch
        first = [
            head_copy(part.at[g, diagonal], staged.at[g], p_send.at[g], p_recv.at[g], partner)
            for g in range(groups)
        ]
        second = [
            head_copy(part.at[g, partner], flank.at[g], q_send.at[g], q_recv.at[g], partner)
            for g in range(groups)
        ]
        third = [
            head_copy(summed.at[g], crossed.at[g], x_send.at[g], x_recv.at[g], across)
            for g in range(groups)
        ]

        def relay(g):
            first[g].wait_recv()
            summed[g] = (
                part[g, across].astype(jnp.float32) + staged[g].astype(jnp.float32)
            ).astype(jnp.bfloat16)
            third[g].start()

        for g in range(groups):
            produce(g)
            first[g].start()
            second[g].start()
            if g > 0:
                relay(g - 1)
        relay(groups - 1)
        for g in range(groups):
            second[g].wait_recv()
            third[g].wait_recv()
            conclude(g, [flank[g], crossed[g]])
        sent = sent + first + second + third
    else:
        landed, r_send, r_recv = scratch
        moves = []
        for g in range(groups):
            produce(g)
            move = [
                head_copy(part.at[g, peer], landed.at[p, g], r_send.at[p, g], r_recv.at[p, g], peer)
                for p, peer in enumerate(head_peers)
            ]
            for copy in move:
                copy.start()
            moves.append(move)
        for g in range(groups):
            for copy in moves[g]:
                copy.wait_recv()
            conclude(g, [landed[p, g] for p in range(n - 1)])
        sent = sent + [copy for move in moves for copy in move]

    for copy in sent:
        copy.wait_send()
    for slot in range(slots):

        @pl.when(gives[slot])
        def _():
            for j in range(2 * per_part):
                halo_copy(slot, j).wait_send()


def quad_kernel(
    peers,
    x_ref, insigns_ref, qscale_ref, qsign_ref, listed_ref, osign_ref, oscale_ref, outsign_ref,
    plane_mat_ref, mat_ref, pscale_ref, pmat_ref, codes_ref, ocodes_ref,
    out_ref,
    early_x, late_x, words, early_w, late_w, acc, eoff, offs, pm, lines, insigns, kv, queries, near,
    owords, oweights, num, tot, own_mask, near_mask, rotated, ooff, part, staged, summed, flank, crossed,
    word_sem, oword_sem, a_send, a_recv, f_send, f_recv, b_send, b_recv, halo_send, halo_recv,
    p_send, p_recv, r_send, r_recv, q_send, q_recv, x_send, x_recv,
):
    me = lax.axis_index("head")
    row = lax.axis_index("height")
    rows, width = x_ref.shape
    count, _, cols = words.shape
    per_part = count // 3
    per_chunk = cols // HD
    local = per_part * cols
    depth = width // PLANES
    groups, gcols = part.shape[0], part.shape[3]
    steps = rows // TILE
    unit = part.shape[2]
    heads = local // HD
    chip, core = me // 2, me % 2
    partner = me + 1 - 2 * core
    across = (me + 2) % 4
    diagonal = (partner + 2) % 4
    distances = (1, -1)

    def tile_at(step):
        return chip * step + (1 - chip) * (steps - 1 - step)

    def fetch(j):
        return pltpu.make_async_copy(
            codes_ref.at[(j // per_part + 1) % 3, :, pl.ds(pl.multiple_of(j % per_part * cols, HD), cols)],
            words.at[j],
            word_sem.at[j],
        )

    for j in range(count):
        fetch(j).start()
    fetch_out = pltpu.make_async_copy(ocodes_ref, owords, oword_sem)
    fetch_out.start()

    barrier = pltpu.get_barrier_semaphore()
    gives = [jnp.logical_and(row + d >= 0, row + d < peers) for d in distances]
    takes = [jnp.logical_and(row - d >= 0, row - d < peers) for d in distances]
    for peer in (partner, across, diagonal):
        pl.semaphore_signal(barrier, inc=1, device_id={"head": peer}, device_id_type=MESH)
    greeted = jnp.int32(3)
    for slot, distance in enumerate(distances):

        @pl.when(gives[slot])
        def _():
            pl.semaphore_signal(
                barrier, inc=1, device_id={"height": row + distance}, device_id_type=MESH
            )

        greeted = greeted + jnp.where(gives[slot], 1, 0)

    for shard in range(4):
        for block in range(width // HAD):
            lanes = slice(block * HAD, (block + 1) * HAD)
            line = signed(insigns_ref[shard * width + block * HAD : shard * width + (block + 1) * HAD])
            insigns[shard, :, lanes] = jnp.broadcast_to(line[None, :], (8, HAD))
    for step in reversed(range(steps)):
        start = pl.multiple_of(tile_at(step) * TILE, TILE)
        for block in range(width // HAD):
            lanes = slice(block * HAD, (block + 1) * HAD)
            plain = x_ref[pl.ds(start, TILE), lanes] * insigns[me, 0:1, lanes].astype(jnp.bfloat16)
            spun = dot(plain, plane_mat_ref[...])
            early_x[0, step, :, lanes] = (spun * pscale_ref[...]).astype(jnp.bfloat16)

    def head_copy(src, dst, send, recv, peer):
        return pltpu.make_async_remote_copy(
            src, dst, send, recv, device_id={"head": peer}, device_id_type=MESH
        )

    crossing = [
        head_copy(early_x.at[0, steps - 1 - i], late_x.at[0, i], a_send.at[i], a_recv.at[i], across)
        for i in range(steps)
    ]
    relays = [
        head_copy(late_x.at[0, i], late_x.at[1, i], f_send.at[i], f_recv.at[i], partner)
        for i in range(steps)
    ]
    beside = head_copy(early_x.at[0], early_x.at[1], b_send, b_recv, partner)
    pl.semaphore_wait(barrier, greeted)
    for copy in crossing:
        copy.start()
    beside.start()

    for block in range(width // HAD):
        pm[block * HAD : (block + 1) * HAD, :] = pmat_ref[...]
    for j in range(count):
        source = (j // per_part + 1) % 3
        spots = slice(j % per_part * cols, (j % per_part + 1) * cols)
        scale = qscale_ref[source : source + 1, spots] * (width * 4) ** -0.5
        sign = signed(qsign_ref[source : source + 1, spots]) * HAD**-0.5
        lines[j, 0:8, :] = jnp.broadcast_to(scale, (8, cols))
        lines[j, 8:16, :] = jnp.broadcast_to(sign, (8, cols))
    for slot in range(2):

        @pl.when(jnp.logical_not(takes[slot]))
        def _():
            near[slot] = jnp.zeros(near.shape[1:], near.dtype)

    def listed_mask(step, ids):
        tile = tile_at(step)
        hit = ids == listed_ref[tile, 0, 0]
        for entry in range(1, listed_ref.shape[2]):
            hit = jnp.logical_or(hit, ids == listed_ref[tile, 0, entry])
        return jnp.where(hit, 1.0, 0.0)

    own_ids = tile_at(lax.broadcasted_iota(jnp.int32, (8, rows), 1) // TILE) + row * steps
    for step in range(steps):
        own_mask[step] = listed_mask(step, own_ids)
    side = lax.broadcasted_iota(jnp.int32, (8, 2 * TILE), 1) // TILE
    side_row = row - 1 + 2 * side
    for s in range(steps):
        for step in range(steps):
            if abs(s - step) < 2:
                near_mask[s, step] = listed_mask(step, side_row * steps + tile_at(s))

    shards = [me, partner, across, diagonal]

    def unpack_role(j, role, target):
        for block in range(depth // GROUP):
            start = pl.multiple_of(shards[role] * depth + block * GROUP, GROUP)
            block_words = words[j, pl.ds(start, GROUP), :]
            for k in range(PLANES):
                spot = block * HAD + k * GROUP
                plane = (block_words & (3 << (2 * k))).astype(jnp.float32).astype(jnp.bfloat16)
                target[role % 2, spot : spot + GROUP, :] = plane

    def prepare(j):
        fetch(j).wait()
        for role in range(2):
            unpack_role(j, role, early_w)
        total = dot(early_x[0].reshape(rows, width), early_w[0])
        total = total + dot(early_x[1].reshape(rows, width), early_w[1])
        for role in range(2, 4):
            unpack_role(j, role, late_w.at[j])
        acc[j] = total.reshape(steps, TILE, cols)

    beside.wait_recv()
    total = dot(early_x[0].reshape(rows, width), pm[...])
    total = total + dot(early_x[1].reshape(rows, width), pm[...])
    eoff[...] = total.reshape(steps, TILE, HD)

    def spread(c):
        spots = pl.ds(pl.multiple_of(c * gcols, HD), gcols)
        for block in range(owords.shape[0] // GROUP):
            block_words = owords[block * GROUP : (block + 1) * GROUP, spots]
            for k in range(PLANES):
                spot = block * HAD + k * GROUP
                plane = (block_words & (3 << (2 * k))).astype(jnp.float32).astype(jnp.bfloat16)
                oweights[c, spot : spot + GROUP, :] = plane

    def halo_copy(slot, step, c):
        return pltpu.make_async_remote_copy(
            kv.at[step, c], near.at[slot, step, c],
            halo_send.at[slot, step, c], halo_recv.at[slot, step, c],
            device_id={"height": row + distances[slot]}, device_id_type=MESH,
        )

    def shift_of(over):
        span = slice(over[0], over[-1] + 1)
        size = len(over) * TILE
        late = dot(late_x[0, span].reshape(size, width), pm[...])
        late = late + dot(late_x[1, span].reshape(size, width), pm[...])
        offs[span] = 1.5 * (eoff[span] + late.reshape(len(over), TILE, HD))

    def project(over, kinds):
        span = slice(over[0], over[-1] + 1)
        size = len(over) * TILE

        @pl.loop(0, per_part)
        def _(c):
            for kind in kinds:
                j = kind * per_part + c
                result = acc[j, span].reshape(size, cols)
                result = result + dot(late_x[0, span].reshape(size, width), late_w[j, 0])
                result = result + dot(late_x[1, span].reshape(size, width), late_w[j, 1])
                shift = offs[span].reshape(size, HD)
                stack, factors = [], []
                for head in range(per_chunk):
                    lanes = slice(head * HD, (head + 1) * HD)
                    block = (result[:, lanes] - shift) * lines[j, 0:1, lanes]
                    high = block.astype(jnp.bfloat16)
                    stack += [high, (block - high.astype(jnp.float32)).astype(jnp.bfloat16)]
                    if kind != 1:
                        mean = jnp.mean(block * block, axis=-1, keepdims=True)
                        factors.append(lax.rsqrt(mean + EPSILON))
                spun = dot(jnp.concatenate(stack, axis=0), mat_ref[...])
                for head in range(per_chunk):
                    lanes = slice(head * HD, (head + 1) * HD)
                    at = 2 * head * size
                    value = (spun[at : at + size] + spun[at + size : at + 2 * size]) * lines[j, 8:9, lanes]
                    if kind != 1:
                        value = value * factors[head]
                    value = value.astype(jnp.bfloat16).reshape(len(over), TILE, HD)
                    for k, a in enumerate(over):
                        if kind == 2:
                            queries[a, c, :, lanes] = value[k]
                        else:
                            kv[a, c, kind, :, lanes] = value[k]
            if kinds == (0, 1):
                for slot in range(2):

                    @pl.when(gives[slot])
                    def _():
                        halo_copy(slot, over[0], c).start()

        if kinds == (0, 1):
            for slot in range(2):

                @pl.when(gives[slot])
                def _():
                    for a in over[1:]:
                        for c in range(per_part):
                            halo_copy(slot, a, c).start()

    @pl.loop(0, count - 2)
    def _(j):
        prepare(j)

    crossing[0].wait_recv()
    relays[0].start()

    @pl.loop(count - 2, count)
    def _(j):
        prepare(j)

    relays[0].wait_recv()
    shift_of((0,))
    project((0,), (0, 1))
    crossing[1].wait_recv()
    relays[1].start()
    fetch_out.wait()

    @pl.loop(0, groups)
    def _(c):
        spread(c)

    relays[1].wait_recv()
    crossing[2].wait_recv()
    relays[2].start()
    relays[2].wait_recv()
    shift_of((1, 2))
    project((1, 2), (0, 1))
    project((0, 1, 2), (2,))

    def attend(rows_q, keys, values, mask):
        score = lax.dot_general(
            rows_q, keys, (((1,), (1,)), ((), ())), preferred_element_type=jnp.float32
        )
        weight = jnp.exp(score * HD**-0.5) * mask
        return dot(weight.astype(jnp.bfloat16), values), jnp.sum(weight, axis=-1, keepdims=True)

    def lanes_of(head):
        return slice(head % per_chunk * HD, (head % per_chunk + 1) * HD)

    def broad(masks):
        return jnp.concatenate([jnp.broadcast_to(m[0:1], (TILE, m.shape[1])) for m in masks], axis=0)

    everything = range(steps)
    mask = broad([own_mask[a] for a in everything])
    for head in range(heads):
        c, lanes = head // per_chunk, lanes_of(head)
        found, sums = attend(
            jnp.concatenate([queries[a, c, :, lanes] for a in everything], axis=0),
            jnp.concatenate([kv[a, c, 0, :, lanes] for a in everything], axis=0),
            jnp.concatenate([kv[a, c, 1, :, lanes] for a in everything], axis=0),
            mask,
        )
        num[:, head] = found.reshape(steps, TILE, HD)
        tot[:, head] = jnp.broadcast_to(sums, found.shape).reshape(steps, TILE, HD)

    def near_wait(s):
        for slot in range(2):

            @pl.when(takes[slot])
            def _():
                for c in range(per_part):
                    halo_copy(slot, s, c).wait_recv()

    def near_attend(s, over):
        mask = broad([near_mask[s, a] for a in over])
        for head in range(heads):
            c, lanes = head // per_chunk, lanes_of(head)
            found, sums = attend(
                jnp.concatenate([queries[a, c, :, lanes] for a in over], axis=0),
                jnp.concatenate([near[slot, s, c, 0, :, lanes] for slot in range(2)], axis=0),
                jnp.concatenate([near[slot, s, c, 1, :, lanes] for slot in range(2)], axis=0),
                mask,
            )
            for at, a in enumerate(over):
                span = slice(at * TILE, (at + 1) * TILE)
                num[a, head] = num[a, head] + found[span]
                tot[a, head] = tot[a, head] + sums[span]

    def complete(over):
        for head in range(heads):
            spots = slice(head * HD, (head + 1) * HD)
            attended = jnp.concatenate([num[a, head] / tot[a, head] for a in over], axis=0)
            attended = attended.astype(jnp.bfloat16) * signed(osign_ref[spots])[None, :].astype(jnp.bfloat16)
            spun = (dot(attended, plane_mat_ref[...]) * pscale_ref[...]).astype(jnp.bfloat16)
            for at, a in enumerate(over):
                rotated[a, :, spots] = spun[at * TILE : (at + 1) * TILE]
        for a in over:
            ooff[a] = 1.5 * dot(rotated[a], pm[0:local, :])

    def produce(g, over):
        left = jnp.concatenate([rotated[a] for a in over], axis=0)
        shift = jnp.concatenate([ooff[a] for a in over], axis=0)
        result = dot(left, oweights[g])
        for block in range(gcols // HAD):
            lanes = slice(block * HAD, (block + 1) * HAD)
            spots = slice(g * gcols + block * HAD, g * gcols + (block + 1) * HAD)
            value = (result[:, lanes] - shift) * (oscale_ref[spots] * (local * 4) ** -0.5)[None, :]
            value = value.astype(jnp.bfloat16)
            for at, a in enumerate(over):
                piece = value[at * TILE : (at + 1) * TILE].reshape(TILE // unit, unit, HAD)
                part[g, pl.ds(tile_at(a) * (TILE // unit), TILE // unit), :, lanes] = piece

    first_base = tile_at(0) * (TILE // unit)
    second_base = TILE // unit + (1 - chip) * 2
    own_base = 3 * me

    def cross_copy(g, k, chunk):
        return head_copy(
            summed.at[g, k], crossed.at[g, chunk % 3], x_send.at[g, k], x_recv.at[g, chunk % 3], chunk // 3
        )

    def arrival(g, k):
        return head_copy(summed.at[g, k], crossed.at[g, k], x_send.at[g, k], x_recv.at[g, k], across)

    def add_up(g, k, chunk):
        summed[g, k] = (
            part[g, chunk].astype(jnp.float32) + staged[g, k].astype(jnp.float32)
        ).astype(jnp.bfloat16)
        cross_copy(g, k, chunk).start()

    first = [
        head_copy(
            part.at[g, pl.ds(first_base + 2 * (1 - core), 2)], staged.at[g, pl.ds(0, 2)],
            p_send.at[g], p_recv.at[g], partner,
        )
        for g in range(groups)
    ]
    second = [
        head_copy(
            part.at[g, pl.ds(second_base + 1 - core, 1)], staged.at[g, pl.ds(2, 1)],
            r_send.at[g], r_recv.at[g], partner,
        )
        for g in range(groups)
    ]
    flanks = [
        head_copy(part.at[g, pl.ds(3 * partner, 3)], flank.at[g], q_send.at[g], q_recv.at[g], partner)
        for g in range(groups)
    ]

    def relay_first(g):
        first[g].wait_recv()
        for k in range(2):
            add_up(g, k, first_base + 2 * core + k)

    def relay_second(g):
        second[g].wait_recv()
        add_up(g, 2, second_base + core)

    near_wait(0)
    near_attend(0, (0, 1))
    near_wait(1)
    near_attend(1, (0,))
    complete((0,))
    for g in range(groups):
        produce(g, (0,))
        first[g].start()
        if g > 0:
            relay_first(g - 1)
    relay_first(groups - 1)
    near_attend(1, (1, 2))
    near_wait(2)
    near_attend(2, (1, 2))
    complete((1, 2))
    for g in range(groups):
        produce(g, (1, 2))
        second[g].start()
        flanks[g].start()
        if g > 0:
            relay_second(g - 1)
    relay_second(groups - 1)

    for g in range(groups):
        flanks[g].wait_recv()
        for k in range(3):
            arrival(g, k).wait_recv()
        for block in range(gcols // HAD):
            lanes = slice(block * HAD, (block + 1) * HAD)
            spots = slice(g * gcols + block * HAD, g * gcols + (block + 1) * HAD)
            total = part[g, pl.ds(own_base, 3), :, lanes].astype(jnp.float32)
            total = total + flank[g, :, :, lanes].astype(jnp.float32)
            total = total + crossed[g, :, :, lanes].astype(jnp.float32)
            spun = rotate_split(total.reshape(3 * unit, HAD), mat_ref[...])
            out_ref[:, spots] = (spun * signed(outsign_ref[spots])[None, :]).astype(jnp.bfloat16)

    for copy in crossing + relays + [beside] + first + second + flanks:
        copy.wait_send()
    for g in range(groups):
        for k in range(3):
            arrival(g, k).wait_send()
    for slot in range(2):

        @pl.when(gives[slot])
        def _():
            for step in range(steps):
                for c in range(per_part):
                    halo_copy(slot, step, c).wait_send()


def quad_call(peers, own, in_sign, qkv_codes, qkv_scale, qkv_sign, windows, oin_sign, out_codes, out_scale, out_sign):
    rows, width = own.shape
    local = qkv_scale.shape[1]
    features = out_codes.shape[1]
    cols = 2 * HD
    count = 3 * local // cols
    per_part = count // 3
    inner = qkv_codes.shape[0]
    gcols = 1024
    groups = features // gcols
    steps = rows // TILE
    heads = local // HD
    unit = rows // 12
    dma = pltpu.SemaphoreType.DMA
    bf16, f32 = jnp.bfloat16, jnp.float32
    vmem = pl.BlockSpec(memory_space=pltpu.VMEM)
    anywhere = pl.BlockSpec(memory_space=pl.ANY)
    smem = pl.BlockSpec(memory_space=pltpu.SMEM)
    triple = pltpu.VMEM((groups, 3, unit, gcols), bf16)
    return pl.pallas_call(
        functools.partial(quad_kernel, peers),
        name="layer",
        out_shape=jax.ShapeDtypeStruct((rows // 4, features), bf16),
        in_specs=[vmem] * 4 + [smem] + [vmem] * 7 + [anywhere] * 2,
        out_specs=vmem,
        scratch_shapes=[
            pltpu.VMEM((2, steps, TILE, width), bf16),
            pltpu.VMEM((2, steps, TILE, width), bf16),
            pltpu.VMEM((count, inner, cols), jnp.int32),
            pltpu.VMEM((2, width, cols), bf16),
            pltpu.VMEM((count, 2, width, cols), bf16),
            pltpu.VMEM((count, steps, TILE, cols), f32),
            pltpu.VMEM((steps, TILE, HD), f32),
            pltpu.VMEM((steps, TILE, HD), f32),
            pltpu.VMEM((width, HD), bf16),
            pltpu.VMEM((count, 16, cols), f32),
            pltpu.VMEM((4, 8, width), f32),
            pltpu.VMEM((steps, per_part, 2, TILE, cols), bf16),
            pltpu.VMEM((steps, per_part, TILE, cols), bf16),
            pltpu.VMEM((2, steps, per_part, 2, TILE, cols), bf16),
            pltpu.VMEM(out_codes.shape, jnp.int32),
            pltpu.VMEM((groups, local, gcols), bf16),
            pltpu.VMEM((steps, heads, TILE, HD), f32),
            pltpu.VMEM((steps, heads, TILE, HD), f32),
            pltpu.VMEM((steps, 8, rows), f32),
            pltpu.VMEM((steps, steps, 8, 2 * TILE), f32),
            pltpu.VMEM((steps, TILE, local), bf16),
            pltpu.VMEM((steps, TILE, HD), f32),
            pltpu.VMEM((groups, 12, unit, gcols), bf16),
            triple,
            triple,
            triple,
            triple,
            dma((count,)),
            dma,
            dma((steps,)),
            dma((steps,)),
            dma((steps,)),
            dma((steps,)),
            dma,
            dma,
            dma((2, steps, per_part)),
            dma((2, steps, per_part)),
            dma((groups,)),
            dma((groups,)),
            dma((groups,)),
            dma((groups,)),
            dma((groups,)),
            dma((groups,)),
            dma((groups, 3)),
            dma((groups, 3)),
        ],
        compiler_params=pltpu.CompilerParams(
            collective_id=0, has_side_effects=True, vmem_limit_bytes=VLIMIT
        ),
    )(
        own,
        in_sign,
        qkv_scale,
        qkv_sign,
        jnp.transpose(windows, (1, 0, 2)),
        oin_sign,
        out_scale,
        out_sign,
        plane_matrix(),
        plain_matrix(),
        plane_scale(),
        power_matrix(),
        jnp.transpose(qkv_codes, (1, 0, 2)),
        out_codes,
    )


def on_device(
    n,
    peers,
    tokens,
    in_sign,
    qkv_codes,
    qkv_scale,
    qkv_sign,
    windows,
    oin_sign,
    out_codes,
    out_scale,
    out_sign,
):
    own = tokens[0]
    rows, width = own.shape
    local = qkv_scale.shape[1]
    features = out_codes.shape[1]
    fitting = rows == 3 * TILE and local % (2 * HD) == 0 and features % 1024 == 0
    if n == 4 and peers <= HROWS and fitting:
        return quad_call(
            peers, own, in_sign, qkv_codes, qkv_scale, qkv_sign, windows,
            oin_sign, out_codes, out_scale, out_sign,
        )[None]
    reach = (1,) if peers <= HROWS else (1, HROWS - 1, HROWS, HROWS + 1)
    distances = tuple(d for r in reach if r < peers for d in (r, -r))
    slots = len(distances)
    cols = 256 if local % 256 == 0 else HD
    count = 3 * local // cols
    per_part = count // 3
    inner = qkv_codes.shape[0]
    gcols = 1024 if features % 1024 == 0 else HD
    groups = features // gcols
    share = rows // n
    chunks = 4
    dma = pltpu.SemaphoreType.DMA
    grouped = pltpu.VMEM((groups, share, gcols), jnp.bfloat16)
    if n == 4:
        tail = [dma((chunks,))] * 4 + [dma] * 2 + [grouped] * 4 + [dma((groups,))] * 6
    else:
        tail = [dma((n - 1,))] * 2
        tail += [pltpu.VMEM((n - 1, groups, share, gcols), jnp.bfloat16)]
        tail += [dma((n - 1, groups))] * 2
    vmem = pl.BlockSpec(memory_space=pltpu.VMEM)
    anywhere = pl.BlockSpec(memory_space=pl.ANY)
    smem = pl.BlockSpec(memory_space=pltpu.SMEM)
    result = pl.pallas_call(
        functools.partial(layer_kernel, n, peers, distances, cols, gcols),
        name="layer",
        out_shape=jax.ShapeDtypeStruct((share, features), jnp.bfloat16),
        in_specs=[vmem] * 4 + [smem] + [vmem] * 7 + [anywhere] * 2,
        out_specs=vmem,
        scratch_shapes=[
            pltpu.VMEM((n, rows, width), jnp.bfloat16),
            pltpu.VMEM((count, inner, cols), jnp.int32),
            pltpu.VMEM((count, n, width, cols), jnp.bfloat16),
            pltpu.VMEM((count, rows, cols), jnp.float32),
            pltpu.VMEM((rows, HD), jnp.float32),
            pltpu.VMEM((count, rows, cols), jnp.bfloat16),
            pltpu.VMEM((slots, 2 * per_part, rows, cols), jnp.bfloat16),
            pltpu.VMEM(out_codes.shape, jnp.int32),
            pltpu.VMEM((groups, local, gcols), jnp.bfloat16),
            pltpu.VMEM((local // HD, rows, HD), jnp.float32),
            pltpu.VMEM((local // HD, rows, HD), jnp.float32),
            pltpu.VMEM((rows, local), jnp.bfloat16),
            pltpu.VMEM((rows, HD), jnp.float32),
            pltpu.VMEM((count, 16, cols), jnp.float32),
            pltpu.VMEM((n, 8, width), jnp.float32),
            pltpu.VMEM((groups, n, share, gcols), jnp.bfloat16),
            dma((count,)),
            dma,
            dma((slots, 2 * per_part)),
            dma((slots, 2 * per_part)),
        ]
        + tail,
        compiler_params=pltpu.CompilerParams(
            collective_id=0, has_side_effects=True, vmem_limit_bytes=VLIMIT
        ),
    )(
        own,
        in_sign,
        qkv_scale,
        qkv_sign,
        jnp.transpose(windows, (1, 0, 2)),
        oin_sign,
        out_scale,
        out_sign,
        plane_matrix(),
        plain_matrix(),
        plane_scale(),
        plane_power(),
        jnp.transpose(qkv_codes, (1, 0, 2)),
        out_codes,
    )
    return result[None]


def solution(mesh):
    n = mesh.shape["head"]
    peers = mesh.shape["height"]
    return jax.shard_map(
        functools.partial(on_device, n, peers),
        mesh=mesh,
        in_specs=(
            P(("clip", "height"), None, "head"),
            P(),
            P(None, None, "head"),
            P(None, "head"),
            P(None, "head"),
            P(("clip", "height"), None, None),
            P("head"),
            P("head", None),
            P(),
            P(),
        ),
        out_specs=P(("clip", "height"), "head", None),
        check_vma=False,
    )
```
